512 devices in a mesh: fsdp: 64 (over z, x, y_lo), tp: 8 (over y_hi, core).
Axes of the slice: x: 4, y: 8 (y_hi: 4, y_lo: 2; y = y_hi * 2 + y_lo), z: 8, core: 2. Of those that a mesh axis runs over, the one named last changes fastest.
Arguments:
- gate_pre: bfloat16 [8192, 14336], P('fsdp', 'tp'), may hold values from -6 to 6
- up_pre: bfloat16 [8192, 14336], P('fsdp', 'tp'), may hold values from -6 to 6
- down_weight: bfloat16 [14336, 4096], P('tp', 'fsdp'), may hold values from -0.046875 to 0.046875
Outputs:
- mixed: bfloat16 [8192, 4096], P('fsdp', 'tp')
The draws below stay inside these ranges and needn't reach their ends.
All inputs are finite; a program needn't handle non-finite values.
Results may differ from the reference program's by a relative error of at most 0.0049.
Values may be sent and summed in bfloat16 or wider, within the bound.
A program may use at most 64 MiB of HBM per device.

```python
import jax
import jax.numpy as jnp

D = 4096
FF = 14336
TOKENS = 8192


def shard_levels(key, dims, split, least, largest):
    factor_of, own = 1.0, jax.random.fold_in(key, 6)
    for axis_at, shards_of in split:
        steps = jnp.exp(jax.random.uniform(jax.random.fold_in(own, axis_at), (shards_of,), jnp.float32, least / len(split), largest / len(split)))
        factor_of = factor_of * jnp.repeat(steps, dims[axis_at] // shards_of).reshape([-1 if axis == axis_at else 1 for axis in range(len(dims))])
    return factor_of


def normal_values(stream_key, dims, width, reach, pieces=(), dtype=jnp.bfloat16):
    values = width * jax.random.normal(stream_key, dims, jnp.float32)
    if pieces:
        values = values * shard_levels(stream_key, dims, pieces, -0.22, 0.18)
    return jnp.clip(values, -reach, reach).astype(dtype)


def setup_inputs(seed: int = 0) -> dict:
    splits = jax.random.split(jax.random.key(seed), 4)
    gate_pre = normal_values(splits[0], (TOKENS, FF), 1.0, 6.0, ((0, 64), (1, 8)))
    up_pre = normal_values(splits[1], (TOKENS, FF), 1.0, 6.0, ((0, 64), (1, 8)))
    down_weight = normal_values(splits[2], (FF, D), FF ** -0.5, 0.046875, ((0, 8), (1, 64)))
    return dict(gate_pre=gate_pre, up_pre=up_pre, down_weight=down_weight)


def reference(gate_pre, up_pre, down_weight):
    hidden = (jax.nn.silu(gate_pre.astype(jnp.float32)) * up_pre.astype(jnp.float32)).astype(jnp.bfloat16)
    return jnp.dot(hidden, down_weight, preferred_element_type=jnp.float32).astype(jnp.bfloat16)
```

```python
import jax
import jax.numpy as jnp
from jax import lax
from jax.experimental import pallas as pl
from jax.experimental.pallas import tpu as pltpu
from jax.sharding import PartitionSpec as P

MESH = pl.DeviceIdType.MESH
X, Y, Z = 4, 8, 8
ROWS, COLS, HALF = 128, 64, 896
STEPS = 4


def kernel(
    gate_hbm, up_hbm, w_hbm, out_ref,
    gate, up, h_send, a_all, b_all, part, other, out_buf, s_buf, r_buf, x_buf,
    load_sem, wx_sem, ax_sem, x_sem, xf_sem, z_sem, c_sem, y_sem, f_sem,
):
    f, t = lax.axis_index("fsdp"), lax.axis_index("tp")
    x, q, z = (f // 2) % X, f % 2, f // (2 * X)
    y, c = (t // 2) * 2 + q, t % 2
    p = 1 - q

    def at(x, y, z, c):
        return (z * 2 * X + x * 2 + y % 2, (y // 2) * 2 + c)

    right, left = at((x + 1) % X, y, z, c), at((x + 3) % X, y, z, c)
    across = at((x + 2) % X, y, z, c)
    north, south = at(x, (y + 1) % Y, z, c), at(x, (y + 7) % Y, z, c)
    ahead, behind = at(x, y, (z + 1) % Z, c), at(x, y, (z + 7) % Z, c)
    twin = at(x, y, z, 1 - c)
    mate = at(x, y + 1 - 2 * q, z, c)

    def send(src, dst, sems, device):
        copy = pltpu.make_async_remote_copy(
            src_ref=src, dst_ref=dst, send_sem=sems.at[0], recv_sem=sems.at[1],
            device_id=device, device_id_type=MESH,
        )
        copy.start()
        return copy

    mine = pl.ds(pl.multiple_of(q * HALF, 128), HALF)
    theirs = pl.ds(pl.multiple_of(p * HALF, 128), HALF)

    def a_at(x, q, start=0, size=ROWS):
        return a_all.at[q, pl.ds(pl.multiple_of(x * ROWS + start, 16), size)]

    def b_at(z, q, start=0, size=COLS):
        return b_all.at[pl.ds(pl.multiple_of((z * 2 + q) * COLS + start, 16), size)]

    loads = [
        pltpu.make_async_copy(w_hbm.at[:, mine], b_at(z, q), load_sem.at[0]),
        pltpu.make_async_copy(gate_hbm.at[:, theirs], gate.at[1], load_sem.at[1]),
        pltpu.make_async_copy(up_hbm.at[:, theirs], up.at[1], load_sem.at[2]),
        pltpu.make_async_copy(gate_hbm.at[:, mine], gate.at[0], load_sem.at[3]),
        pltpu.make_async_copy(up_hbm.at[:, mine], up.at[0], load_sem.at[4]),
    ]
    for load in loads:
        load.start()

    barrier = pltpu.get_barrier_semaphore()
    for peer in (right, left, across, north, south, ahead, behind, twin):
        pl.semaphore_signal(barrier, inc=1, device_id=peer, device_id_type=MESH)
    pl.semaphore_wait(barrier, 8)

    copies = []

    w_swap = send(w_hbm.at[:, theirs], b_at(z, q), wx_sem, mate)

    def z_hop(step, piece):
        who = q if piece == 0 else p
        cut = COLS if step < STEPS - 1 else COLS // 2
        fwd, back = (z + Z - step) % Z, (z + step) % Z
        up_src = b_at(fwd, who, 0, cut)
        down_src = b_at(back, who, COLS - cut, cut)
        return (
            send(up_src, up_src, z_sem.at[0, step, piece], ahead),
            send(down_src, down_src, z_sem.at[1, step, piece], behind),
        )

    def x_hop(piece):
        src = a_at(x, q if piece == 0 else p)
        return send(src, src, x_sem.at[0, piece], right), send(src, src, x_sem.at[1, piece], left)

    def x_forward(piece):
        who = q if piece == 0 else p
        fwd = a_at((x + 3) % X, who, 0, ROWS // 2)
        back = a_at((x + 1) % X, who, ROWS // 2, ROWS // 2)
        return send(fwd, fwd, xf_sem.at[0, piece], right), send(back, back, xf_sem.at[1, piece], left)

    def landed(pair):
        for copy in pair:
            copy.wait_recv()

    loads[0].wait()
    z0a = z_hop(0, 0)

    def act(i):
        g = gate[i].astype(jnp.float32)
        return (g / (1.0 + jnp.exp(-g)) * up[i].astype(jnp.float32)).astype(jnp.bfloat16)

    loads[1].wait()
    loads[2].wait()
    h_send[...] = act(1)
    a_swap = send(h_send, a_at(x, q), ax_sem, mate)
    loads[3].wait()
    loads[4].wait()
    a_at(x, q)[...] = act(0)
    x0a = x_hop(0)
    w_swap.wait_recv()
    z0b = z_hop(0, 1)
    landed(z0a)
    z1a = z_hop(1, 0)
    landed(z0b)
    z1b = z_hop(1, 1)
    a_swap.wait_recv()
    x0b = x_hop(1)
    landed(z1a)
    z2a = z_hop(2, 0)
    landed(x0a)
    x1a = x_forward(0)
    landed(z1b)
    z2b = z_hop(2, 1)
    landed(z2a)
    z3a = z_hop(3, 0)
    landed(x0b)
    x1b = x_forward(1)
    landed(z2b)
    z3b = z_hop(3, 1)
    for pair in (x1a, x1b, z3a, z3b):
        landed(pair)
    for pair in (z0a, z0b, z1a, z1b, z2a, z2b, z3a, z3b, x0a, x0b, x1a, x1b):
        for copy in pair:
            copy.wait_send()
    w_swap.wait_send()
    a_swap.wait_send()

    def target(i):
        odd = i % 2
        return (y + 4 + (1 - odd) * (i // 2) - odd * ((i + 1) // 2)) % Y

    def core_copy(to):
        return pltpu.make_async_remote_copy(
            src_ref=part.at[1 - c, to], dst_ref=other.at[to],
            send_sem=c_sem.at[0, to], recv_sem=c_sem.at[1, to],
            device_id=twin, device_id_type=MESH,
        )

    def product(i, carry):
        to = target(i)
        b = b_all[pl.ds(pl.multiple_of((to // 2) * 256, 256), 256)]
        r = lax.dot_general(
            a_all[to % 2], b, (((1,), (1,)), ((), ())), preferred_element_type=jnp.float32
        )
        part[0, to] = r[:, :128]
        part[1, to] = r[:, 128:]
        core_copy(to).start()
        return carry

    lax.fori_loop(0, Y, product, 0)

    def own(to, start=0, size=4 * ROWS):
        rows = pl.ds(start, size)
        return part[c, to, rows] + other[to, rows]

    half = 2 * ROWS
    far = (y + 4) % Y
    core_copy(far).wait_recv()
    s_buf[0, 0, :half] = own(far, 0, half).astype(jnp.bfloat16)
    s_buf[1, 0, half:] = own(far, half, half).astype(jnp.bfloat16)

    def y_hop(way, step):
        rows = pl.ds(way * half, half) if step == 0 else pl.ds(0, 2 * half)
        return send(
            s_buf.at[way, step, rows], r_buf.at[way, step, rows],
            y_sem.at[way, step], north if way == 0 else south,
        )

    hops = [y_hop(0, 0), y_hop(1, 0)]
    for step in range(1, STEPS):
        for way in range(2):
            to = (y + (STEPS - step if way == 0 else Y - STEPS + step)) % Y
            core_copy(to).wait_recv()
            came = hops[2 * (step - 1) + way]
            came.wait_recv()
            if step == 1:
                with_half, without = (0, half) if way == 0 else (half, 0)
                s_buf[way, step, with_half : with_half + half] = (
                    own(to, with_half, half)
                    + r_buf[way, 0, with_half : with_half + half].astype(jnp.float32)
                ).astype(jnp.bfloat16)
                s_buf[way, step, without : without + half] = own(to, without, half).astype(jnp.bfloat16)
            else:
                s_buf[way, step] = (own(to) + r_buf[way, step - 1].astype(jnp.float32)).astype(jnp.bfloat16)
            hops.append(y_hop(way, step))
    core_copy(y).wait_recv()
    hops[-2].wait_recv()
    hops[-1].wait_recv()
    total = own(y) + r_buf[0, STEPS - 1].astype(jnp.float32) + r_buf[1, STEPS - 1].astype(jnp.float32)
    x_buf[...] = total.astype(jnp.bfloat16).reshape(X, ROWS, 128)

    outs = []
    for i, device in ((1, right), (3, left), (2, across)):
        outs.append(send(x_buf.at[(x + i) % X], out_buf.at[x], f_sem.at[i], device))
    keep = pltpu.make_async_copy(x_buf.at[x], out_buf.at[x], load_sem.at[0])
    keep.start()
    keep.wait()
    for copy in outs:
        copy.wait_recv()
    for i in range(X):
        out_ref[:, i * 128 : (i + 1) * 128] = out_buf[i]
    for copy in outs + hops:
        copy.wait_send()

    def drain(i, carry):
        core_copy(i).wait_send()
        return carry

    lax.fori_loop(0, Y, drain, 0)


def shards(gate_pre, up_pre, down_weight):
    dma = pltpu.SemaphoreType.DMA
    bf16, f32 = jnp.bfloat16, jnp.float32
    return pl.pallas_call(
        kernel,
        out_shape=jax.ShapeDtypeStruct((ROWS, 512), bf16),
        in_specs=[pl.BlockSpec(memory_space=pl.ANY)] * 3,
        out_specs=pl.BlockSpec(memory_space=pltpu.VMEM),
        scratch_shapes=[
            pltpu.VMEM((2, ROWS, HALF), bf16),
            pltpu.VMEM((2, ROWS, HALF), bf16),
            pltpu.VMEM((ROWS, HALF), bf16),
            pltpu.VMEM((2, X * ROWS, HALF), bf16),
            pltpu.VMEM((Z * 2 * COLS, HALF), bf16),
            pltpu.VMEM((2, Y, X * ROWS, 128), f32),
            pltpu.VMEM((Y, X * ROWS, 128), f32),
            pltpu.VMEM((X, ROWS, 128), bf16),
            pltpu.VMEM((2, STEPS, X * ROWS, 128), bf16),
            pltpu.VMEM((2, STEPS, X * ROWS, 128), bf16),
            pltpu.VMEM((X, ROWS, 128), bf16),
            dma((5,)),
            dma((2,)),
            dma((2,)),
            dma((2, 2, 2)),
            dma((2, 2, 2)),
            dma((2, STEPS, 2, 2)),
            dma((2, Y)),
            dma((2, STEPS, 2)),
            dma((X, 2)),
        ],
        compiler_params=pltpu.CompilerParams(
            collective_id=0, has_side_effects=True, vmem_limit_bytes=48 << 20
        ),
        name="down_projection",
    )(gate_pre, up_pre, down_weight.T)


def solution(mesh):
    return jax.shard_map(
        shards,
        mesh=mesh,
        in_specs=(P("fsdp", "tp"), P("fsdp", "tp"), P("tp", "fsdp")),
        out_specs=P("fsdp", "tp"),
        check_vma=False,
    )
```

```python
import jax
import jax.numpy as jnp
from jax import lax
from jax.experimental import pallas as pl
from jax.experimental.pallas import tpu as pltpu
from jax.sharding import PartitionSpec as P

MESH = pl.DeviceIdType.MESH
X, Y, Z = 4, 8, 8
ROWS, COLS, HALF = 128, 64, 896


def kernel(
    gate_hbm, up_hbm, w_hbm, out_ref,
    gate, up, h_send, a_all, b_all, part, other, s_buf, r_buf, f_buf, fin,
    load_sem, wx_sem, ax_sem, x_sem, z_sem, c_sem, y_sem, f_sem,
):
    f, t = lax.axis_index("fsdp"), lax.axis_index("tp")
    x, q, z = (f // 2) % X, f % 2, f // (2 * X)
    y, c = (t // 2) * 2 + q, t % 2
    p = 1 - q
    sent = []

    def at(dx=0, dy=0, dz=0, core=c):
        to_x, to_y, to_z = (x + X + dx) % X, (y + Y + dy) % Y, (z + Z + dz) % Z
        return (to_z * 2 * X + to_x * 2 + to_y % 2, (to_y // 2) * 2 + core)

    mate = at(dy=1 - 2 * q)
    twin = at(core=1 - c)

    def send(src, dst, sems, device):
        copy = pltpu.make_async_remote_copy(
            src_ref=src, dst_ref=dst, send_sem=sems.at[0], recv_sem=sems.at[1],
            device_id=device, device_id_type=MESH,
        )
        copy.start()
        sent.append(copy)
        return copy

    mine = pl.ds(pl.multiple_of(q * HALF, 128), HALF)
    theirs = pl.ds(pl.multiple_of(p * HALF, 128), HALF)

    def a_at(x, q, start=0, size=ROWS):
        return a_all.at[q, pl.ds(pl.multiple_of(x * ROWS + start, 16), size)]

    def b_at(z, q, start=0, size=COLS):
        return b_all.at[pl.ds(pl.multiple_of((z * 2 + q) * COLS + start, 16), size)]

    loads = [
        pltpu.make_async_copy(w_hbm.at[:, mine], b_at(z, q), load_sem.at[0]),
        pltpu.make_async_copy(gate_hbm.at[:, theirs], gate.at[1], load_sem.at[1]),
        pltpu.make_async_copy(up_hbm.at[:, theirs], up.at[1], load_sem.at[2]),
        pltpu.make_async_copy(gate_hbm.at[:, mine], gate.at[0], load_sem.at[3]),
        pltpu.make_async_copy(up_hbm.at[:, mine], up.at[0], load_sem.at[4]),
    ]
    for load in loads:
        load.start()

    barrier = pltpu.get_barrier_semaphore()
    peers = [at(dx, dy) for dx in range(X) for dy in range(-2, 3) if (dx, dy) != (0, 0)]
    peers += [at(dz=dz) for dz in (-2, -1, 1, 2)] + [twin]
    for peer in peers:
        pl.semaphore_signal(barrier, inc=1, device_id=peer, device_id_type=MESH)
    pl.semaphore_wait(barrier, len(peers))

    part_w = COLS // 2
    w_swap = [
        send(
            w_hbm.at[pl.ds(i * part_w, part_w), theirs], b_at(z, q, i * part_w, part_w),
            wx_sem.at[i], mate,
        )
        for i in range(2)
    ]

    def z_hop(step, piece):
        who = q if piece < 2 else p
        hop, far = (2, 2) if step == 3 else (1, step)
        size = part_w // 2 if step == 3 else part_w
        start = (piece % 2) * part_w
        ahead = b_at((z + Z - far) % Z, who, start, size)
        behind = b_at((z + far) % Z, who, start + part_w - size, size)
        return [
            send(ahead, ahead, z_sem.at[0, step, piece], at(dz=hop)),
            send(behind, behind, z_sem.at[1, step, piece], at(dz=-hop)),
        ]

    def x_hop(piece):
        src = a_at(x, q if piece < 2 else p, (piece % 2) * 64, 64)
        return [send(src, src, x_sem.at[i, piece], at(dx=d)) for i, d in enumerate((1, 3, 2))]

    def landed(copies):
        for copy in copies:
            copy.wait_recv()

    def act(i):
        g = gate[i].astype(jnp.float32)
        return (g / (1.0 + jnp.exp(-g)) * up[i].astype(jnp.float32)).astype(jnp.bfloat16)

    zs, xs = {}, {}
    loads[0].wait()
    for i in (0, 1):
        zs[0, i] = z_hop(0, i)
    loads[1].wait()
    loads[2].wait()
    h_send[...] = act(1)
    a_swap = [
        send(h_send.at[pl.ds(i * 64, 64)], a_at(x, q, i * 64, 64), ax_sem.at[i], mate)
        for i in range(2)
    ]
    loads[3].wait()
    loads[4].wait()
    a_at(x, q)[...] = act(0)
    for i in (0, 1):
        xs[i] = x_hop(i)
    for i in (2, 3):
        w_swap[i - 2].wait_recv()
        zs[0, i] = z_hop(0, i)
    for i in (0, 1):
        landed(zs[0, i])
        zs[1, i] = z_hop(1, i)
    for i in (2, 3):
        a_swap[i - 2].wait_recv()
        xs[i] = x_hop(i)
    for i in (2, 3):
        landed(zs[0, i])
        zs[1, i] = z_hop(1, i)
    for pair in ((0, 1), (2, 3)):
        for i in pair:
            landed(zs[1, i])
            zs[3, i] = z_hop(3, i)
            zs[2, i] = z_hop(2, i)
    for i in range(4):
        landed(xs[i])
        landed(zs[2, i])
        landed(zs[3, i])

    def core_copy(to):
        return pltpu.make_async_remote_copy(
            src_ref=part.at[1 - c, to], dst_ref=other.at[to],
            send_sem=c_sem.at[0, to], recv_sem=c_sem.at[1, to],
            device_id=twin, device_id_type=MESH,
        )

    def product(i, carry):
        odd = i % 2
        to = (y + 4 + (1 - odd) * (i // 2) - odd * ((i + 1) // 2)) % Y
        b = b_all[pl.ds(pl.multiple_of((to // 2) * 256, 256), 256)]
        r = lax.dot_general(
            a_all[to % 2], b, (((1,), (1,)), ((), ())), preferred_element_type=jnp.float32
        )
        part[0, to] = r[:, :128]
        part[1, to] = r[:, 128:]
        core_copy(to).start()
        return carry

    lax.fori_loop(0, Y, product, 0)

    def own(to, start=0, size=X * ROWS):
        rows = pl.ds(start, size)
        return part[c, to, rows] + other[to, rows]

    half = 2 * ROWS

    def settle(offset):
        to = (y + Y + offset) % Y
        core_copy(to).wait_recv()
        return to

    to = settle(4)
    s_buf[0] = own(to).astype(jnp.bfloat16)
    far = [
        send(s_buf.at[0, pl.ds(i * half, half)], r_buf.at[0, pl.ds(i * half, half)], y_sem.at[i], at(dy=d))
        for i, d in enumerate((2, -2))
    ]
    near = {}
    for i, offset in ((1, 3), (2, -3)):
        to = settle(offset)
        s_buf[i] = own(to).astype(jnp.bfloat16)
        near[i] = send(s_buf.at[i], r_buf.at[i], y_sem.at[1 + i], at(dy=1 if offset > 0 else -1))

    lasts = []

    def final(offset):
        for k in (2, 1, 3, 0):
            if (k, offset) != (0, 0):
                i = (x + k) % X
                lasts.append(
                    send(f_buf.at[offset + 2, i], fin.at[offset + 2, x], f_sem.at[offset + 2, k], at(dx=k, dy=offset))
                )

    for offset in (1, -1):
        to = settle(offset)
        f_buf[offset + 2] = own(to).astype(jnp.bfloat16).reshape(X, ROWS, 128)
        final(offset)
    for i, offset in ((0, 2), (1, -2)):
        to = settle(offset)
        far[i].wait_recv()
        near[1 + i].wait_recv()
        total = own(to) + r_buf[1 + i].astype(jnp.float32)
        mid = r_buf[0, i * half : (i + 1) * half].astype(jnp.float32)
        with_far = (total[i * half : (i + 1) * half] + mid).astype(jnp.bfloat16)
        rest = total[(1 - i) * half : (2 - i) * half].astype(jnp.bfloat16)
        f_buf[offset + 2, 2 * i : 2 * i + 2] = with_far.reshape(2, ROWS, 128)
        f_buf[offset + 2, 2 - 2 * i : 4 - 2 * i] = rest.reshape(2, ROWS, 128)
        final(offset)
    to = settle(0)
    f_buf[2] = own(to).astype(jnp.bfloat16).reshape(X, ROWS, 128)
    final(0)
    fin[2, x] = f_buf[2, x]
    for copy in lasts:
        copy.wait_recv()
    for i in range(X):
        total = fin[0, i].astype(jnp.float32)
        for j in range(1, 5):
            total = total + fin[j, i].astype(jnp.float32)
        out_ref[:, i * 128 : (i + 1) * 128] = total.astype(jnp.bfloat16)
    for copy in sent:
        copy.wait_send()
    for i in range(Y):
        core_copy(i).wait_send()


def shards(gate_pre, up_pre, down_weight):
    dma = pltpu.SemaphoreType.DMA
    bf16, f32 = jnp.bfloat16, jnp.float32
    return pl.pallas_call(
        kernel,
        out_shape=jax.ShapeDtypeStruct((ROWS, 512), bf16),
        in_specs=[pl.BlockSpec(memory_space=pl.ANY)] * 3,
        out_specs=pl.BlockSpec(memory_space=pltpu.VMEM),
        scratch_shapes=[
            pltpu.VMEM((2, ROWS, HALF), bf16),
            pltpu.VMEM((2, ROWS, HALF), bf16),
            pltpu.VMEM((ROWS, HALF), bf16),
            pltpu.VMEM((2, X * ROWS, HALF), bf16),
            pltpu.VMEM((Z * 2 * COLS, HALF), bf16),
            pltpu.VMEM((2, Y, X * ROWS, 128), f32),
            pltpu.VMEM((Y, X * ROWS, 128), f32),
            pltpu.VMEM((3, X * ROWS, 128), bf16),
            pltpu.VMEM((3, X * ROWS, 128), bf16),
            pltpu.VMEM((5, X, ROWS, 128), bf16),
            pltpu.VMEM((5, X, ROWS, 128), bf16),
            dma((5,)),
            dma((2, 2)),
            dma((2, 2)),
            dma((3, 4, 2)),
            dma((2, 4, 4, 2)),
            dma((2, Y)),
            dma((4, 2)),
            dma((5, X, 2)),
        ],
        compiler_params=pltpu.CompilerParams(
            collective_id=0, has_side_effects=True, vmem_limit_bytes=55000 * 1024
        ),
        name="down_projection",
    )(gate_pre, up_pre, down_weight.T)


def solution(mesh):
    return jax.shard_map(
        shards,
        mesh=mesh,
        in_specs=(P("fsdp", "tp"), P("fsdp", "tp"), P("tp", "fsdp")),
        out_specs=P("fsdp", "tp"),
        check_vma=False,
    )
```

```python
import jax
import jax.numpy as jnp
from jax import lax
from jax.experimental import pallas as pl
from jax.experimental.pallas import tpu as pltpu
from jax.sharding import PartitionSpec as P

MESH = pl.DeviceIdType.MESH
X, Y, Z = 4, 8, 8
ROWS, COLS, HALF = 128, 64, 896


def kernel(
    gate_hbm, up_hbm, w_hbm, out_ref,
    gate, up, h_send, a_all, b_all, part, other, s_buf, r_buf, f_buf, fin,
    load_sem, wx_sem, ax_sem, x_sem, z_sem, c_sem, y_sem, f_sem, relay,
):
    rem, div = lax.rem, lax.div
    f, t = lax.axis_index("fsdp"), lax.axis_index("tp")
    x, q, z = rem(div(f, 2), X), rem(f, 2), div(f, 2 * X)
    y, c = div(t, 2) * 2 + q, rem(t, 2)
    p = 1 - q
    sent = []

    def at(dx=0, dy=0, dz=0, core=c):
        to_x = x if isinstance(dx, int) and dx == 0 else rem(x + (X + dx), X)
        to_y = y if isinstance(dy, int) and dy == 0 else rem(y + (Y + dy), Y)
        to_z = z if isinstance(dz, int) and dz == 0 else rem(z + (Z + dz), Z)
        return (to_z * (2 * X) + to_x * 2 + rem(to_y, 2), div(to_y, 2) * 2 + core)

    mate = at(dy=1 - 2 * q)
    twin = at(core=1 - c)

    def copy_to(src, dst, sems, device):
        return pltpu.make_async_remote_copy(
            src_ref=src, dst_ref=dst, send_sem=sems.at[0], recv_sem=sems.at[1],
            device_id=device, device_id_type=MESH,
        )

    def send(*args):
        copy = copy_to(*args)
        copy.start()
        sent.append(copy)
        return copy

    def each(n, body, start=0):
        def step(i, carry):
            body(i)
            return carry

        lax.fori_loop(start, n, step, 0)

    mine = pl.ds(pl.multiple_of(q * HALF, 128), HALF)
    theirs = pl.ds(pl.multiple_of(p * HALF, 128), HALF)

    def a_at(x, q, start=0, size=ROWS):
        return a_all.at[q, pl.ds(pl.multiple_of(x * ROWS + start, 16), size)]

    def b_at(z, q, start=0, size=COLS):
        return b_all.at[pl.ds(pl.multiple_of((z * 2 + q) * COLS + start, 16), size)]

    loads = [
        pltpu.make_async_copy(w_hbm.at[:, mine], b_at(z, q), load_sem.at[0]),
        pltpu.make_async_copy(gate_hbm.at[:, theirs], gate.at[1], load_sem.at[1]),
        pltpu.make_async_copy(up_hbm.at[:, theirs], up.at[1], load_sem.at[2]),
        pltpu.make_async_copy(gate_hbm.at[:, mine], gate.at[0], load_sem.at[3]),
        pltpu.make_async_copy(up_hbm.at[:, mine], up.at[0], load_sem.at[4]),
    ]
    for load in loads:
        load.start()

    barrier = pltpu.get_barrier_semaphore()

    def greet(device):
        pl.semaphore_signal(barrier, inc=1, device_id=device, device_id_type=MESH)

    up_z, down_z = at(dz=1), at(dz=-1)
    greet(up_z)
    greet(down_z)
    greet(at(dy=1))
    greet(at(dy=-1))
    greet(at(1))
    greet(at(3))
    greet(twin)
    def act(i, dst):
        def rows(r):
            at_rows = pl.ds(pl.multiple_of(r * 16, 16), 16)
            g = gate[i, at_rows].astype(jnp.float32)
            h = g / (1.0 + jnp.exp(-g)) * up[i, at_rows].astype(jnp.float32)
            dst[at_rows] = h.astype(jnp.bfloat16)

        each(ROWS // 16, rows)

    loads[1].wait()
    loads[2].wait()
    act(1, h_send)
    loads[3].wait()
    loads[4].wait()
    act(0, a_at(x, q))
    pl.semaphore_wait(barrier, 7)
    for dy in (1, -1):
        pl.semaphore_signal(relay, inc=1, device_id=at(dy=dy), device_id_type=MESH)

    cut = COLS // 2
    w_swap = [
        send(w_hbm.at[pl.ds(i * cut, cut), theirs], b_at(z, q, i * cut, cut), wx_sem.at[i], mate)
        for i in range(2)
    ]

    def z_hop(step, piece):
        who = p if piece > 1 else q
        far, size = (2, cut // 2) if step == 3 else (step, cut)
        start = piece % 2 * cut
        ahead = b_at(rem(z + (Z - far), Z), who, start, size)
        behind = b_at(rem(z + far, Z), who, start + cut - size, size)
        return [
            send(ahead, ahead, z_sem.at[0, step, piece], at(dz=2) if step == 3 else up_z),
            send(behind, behind, z_sem.at[1, step, piece], at(dz=-2) if step == 3 else down_z),
        ]

    right, left = at(1), at(3)

    def x_hop(piece):
        src = a_at(x, p if piece > 1 else q, piece % 2 * 64, 64)
        return [send(src, src, x_sem.at[i, piece], d) for i, d in enumerate((right, left))]

    def x_on(piece):
        i = piece % 2
        src = a_at(rem(x + (3 if i == 0 else 1), X), p if piece > 1 else q, i * 64, 64)
        return [send(src, src, x_sem.at[2, piece], right if i == 0 else left)]

    def landed(copies):
        for copy in copies:
            copy.wait_recv()

    zs, xs, xo = {}, {}, {}
    loads[0].wait()
    for i in (0, 1):
        zs[0, i] = z_hop(0, i)
    a_swap = [
        send(h_send.at[pl.ds(i * 64, 64)], a_at(x, q, i * 64, 64), ax_sem.at[i], mate) for i in range(2)
    ]
    for i in (0, 1):
        xs[i] = x_hop(i)
    for i in (2, 3):
        w_swap[i - 2].wait_recv()
        zs[0, i] = z_hop(0, i)
    for i in (0, 1):
        landed(zs[0, i])
        zs[1, i] = z_hop(1, i)
    pl.semaphore_wait(relay, 2)
    for i in (2, 3):
        a_swap[i - 2].wait_recv()
        xs[i] = x_hop(i)
    for i in (0, 1):
        landed(xs[i])
        xo[i] = x_on(i)
    for i in (2, 3):
        landed(zs[0, i])
        zs[1, i] = z_hop(1, i)
    for i in (0, 1):
        landed(zs[1, i])
        zs[3, i] = z_hop(3, i)
        zs[2, i] = z_hop(2, i)
    for i in (2, 3):
        landed(xs[i])
        xo[i] = x_on(i)
    for i in (2, 3):
        landed(zs[1, i])
        zs[3, i] = z_hop(3, i)
        zs[2, i] = z_hop(2, i)
    near_z = [copy for i in range(4) for copy in zs[2, i]]
    far_z = [copy for i in range(4) for copy in zs[3, i]]
    for i in range(4):
        landed(xo[i])

    def core_copy(to):
        return copy_to(part.at[1 - c, to], other.at[to], c_sem.at[to], twin)

    def product(i):
        pl.when(i == 5)(lambda: landed(near_z))
        pl.when(i == 7)(lambda: landed(far_z))
        odd = rem(i, 2)
        zz = rem(z + odd * div(i + 1, 2) + (1 - odd) * (Z - div(i, 2)), Z)
        owner, to = rem(zz, 2), div(zz, 2) * 2
        b = b_all[pl.ds(pl.multiple_of(zz * 128, 128), 128)]

        def block(j):
            part[owner, to + j] = lax.dot_general(
                a_all[j], b, (((1,), (1,)), ((), ())), preferred_element_type=jnp.float32
            )

        each(2, block)

        @pl.when(owner != c)
        def _():
            core_copy(to).start()
            core_copy(to + 1).start()

    half = 2 * ROWS

    def settle(offset):
        to = rem(y + Y + offset, Y)
        core_copy(to).wait_recv()
        return to

    def pack(to, dst, start=0, stop=X, extra=()):
        def chunk(k):
            rows = pl.ds(pl.multiple_of(k * ROWS, ROWS), ROWS)
            v = part[c, to, rows] + other[to, rows]
            for e in extra:
                v = v + e[rows].astype(jnp.float32)
            dst[rows] = v.astype(jnp.bfloat16)

        each(stop, chunk, start)

    def far(i):
        rows = pl.ds(i * half, half)
        return copy_to(s_buf.at[0, rows], r_buf.at[0, rows], y_sem.at[i], at(dy=-2 if i else 2))

    def near(i):
        return copy_to(s_buf.at[1 + i], r_buf.at[1 + i], y_sem.at[2 + i], at(dy=-1 if i else 1))

    def when_due(offset, batch, body):
        to = rem(y + Y + offset, Y)
        dz = rem(div(to, 2) * 2 + c + (Z + 2) - z, Z)
        late = (dz > 4).astype(jnp.int32)

        @pl.when(late == batch)
        def _():
            body(to)

    def last(offset, k):
        rows = pl.ds(pl.multiple_of(rem(x + k, X) * ROWS, ROWS), ROWS)
        return copy_to(f_buf.at[offset + 2, rows], fin.at[offset + 2, x], f_sem.at[offset + 2, k], at(k, offset))

    def final(offset):
        each(X, lambda k: last(offset, k).start(), 1 if isinstance(offset, int) and offset == 0 else 0)

    def send_far(to):
        settle(4)
        pack(to, s_buf.at[0])
        far(0).start()
        far(1).start()

    def send_near(i, offset):
        def body(to):
            settle(offset)
            pack(to, s_buf.at[1 + i])
            near(i).start()

        return body

    def send_own(offset):
        def body(to):
            settle(offset)
            pack(to, f_buf.at[offset + 2])
            final(offset)

        return body

    def send_sum(i, offset):
        def body(to):
            settle(offset)
            far(i).wait_recv()
            near(i).wait_recv()
            pack(to, f_buf.at[offset + 2], 2 * i, 2 * i + 2, (r_buf.at[0], r_buf.at[1 + i]))
            pack(to, f_buf.at[offset + 2], 2 - 2 * i, 4 - 2 * i, (r_buf.at[1 + i],))
            final(offset)

        return body

    def batch(b):
        each(5 + 3 * b, product, 5 * b)
        when_due(4, b, send_far)
        when_due(3, b, send_near(0, 3))
        when_due(-3, b, send_near(1, -3))
        for offset in (1, -1, 0):
            when_due(offset, b, send_own(offset))

    each(2, batch)

    def sums(b):
        when_due(2, b, send_sum(0, 2))
        when_due(-2, b, send_sum(1, -2))

    each(2, sums)
    fin[2, x] = f_buf[2, pl.ds(pl.multiple_of(x * ROWS, ROWS), ROWS)]
    for offset in (0, 1, -1, 2, -2):
        each(X, lambda k: last(offset, k).wait_recv(), 0 if offset else 1)

    def add_up(i):
        total = fin[0, i].astype(jnp.float32)
        for j in range(1, 5):
            total = total + fin[j, i].astype(jnp.float32)
        out_ref[:, pl.ds(pl.multiple_of(i * 128, 128), 128)] = total.astype(jnp.bfloat16)

    each(X, add_up)
    for copy in sent + [far(0), far(1), near(0), near(1)]:
        copy.wait_send()
    each(Y, lambda i: core_copy(i).wait_send())
    for offset in (0, 1, -1, 2, -2):
        each(X, lambda k: last(offset, k).wait_send(), 0 if offset else 1)


def shards(gate_pre, up_pre, down_weight):
    dma = pltpu.SemaphoreType.DMA
    bf16, f32 = jnp.bfloat16, jnp.float32
    return pl.pallas_call(
        kernel,
        out_shape=jax.ShapeDtypeStruct((ROWS, 512), bf16),
        in_specs=[pl.BlockSpec(memory_space=pl.ANY)] * 3,
        out_specs=pl.BlockSpec(memory_space=pltpu.VMEM),
        scratch_shapes=[
            pltpu.VMEM((2, ROWS, HALF), bf16),
            pltpu.VMEM((2, ROWS, HALF), bf16),
            pltpu.VMEM((ROWS, HALF), bf16),
            pltpu.VMEM((2, X * ROWS, HALF), bf16),
            pltpu.VMEM((Z * 2 * COLS, HALF), bf16),
            pltpu.VMEM((2, Y, X * ROWS, 128), f32),
            pltpu.VMEM((Y, X * ROWS, 128), f32),
            pltpu.VMEM((3, X * ROWS, 128), bf16),
            pltpu.VMEM((3, X * ROWS, 128), bf16),
            pltpu.VMEM((5, X * ROWS, 128), bf16),
            pltpu.VMEM((5, X, ROWS, 128), bf16),
            dma((5,)),
            dma((2, 2)),
            dma((2, 2)),
            dma((3, 4, 2)),
            dma((2, 4, 4, 2)),
            dma((Y, 2)),
            dma((4, 2)),
            dma((5, X, 2)),
            pltpu.SemaphoreType.REGULAR,
        ],
        compiler_params=pltpu.CompilerParams(
            collective_id=0, has_side_effects=True, vmem_limit_bytes=55000 * 1024
        ),
        name="down_projection",
    )(gate_pre, up_pre, down_weight.T)


def solution(mesh):
    return jax.shard_map(
        shards,
        mesh=mesh,
        in_specs=(P("fsdp", "tp"), P("fsdp", "tp"), P("tp", "fsdp")),
        out_specs=P("fsdp", "tp"),
        check_vma=False,
    )
```

```python
import jax
import jax.numpy as jnp
from jax import lax
from jax.experimental import pallas as pl
from jax.experimental.pallas import tpu as pltpu
from jax.sharding import PartitionSpec as P

MESH = pl.DeviceIdType.MESH
X, Y, Z = 4, 8, 8
ROWS, COLS, HALF = 128, 64, 896


def kernel(
    gate_hbm, up_hbm, w_hbm, out_ref,
    gate, up, h_send, a_all, b_all, part, other, s_buf, r_buf, f_buf, fin,
    load_sem, wx_sem, ax_sem, x_sem, z_sem, c_sem, y_sem, f_sem, relay,
):
    rem, div = lax.rem, lax.div
    f, t = lax.axis_index("fsdp"), lax.axis_index("tp")
    x, q, z = rem(div(f, 2), X), rem(f, 2), div(f, 2 * X)
    y, c = div(t, 2) * 2 + q, rem(t, 2)
    p = 1 - q
    sent = []

    def at(dx=0, dy=0, dz=0, core=c):
        to_x = x if isinstance(dx, int) and dx == 0 else rem(x + (X + dx), X)
        to_y = y if isinstance(dy, int) and dy == 0 else rem(y + (Y + dy), Y)
        to_z = z if isinstance(dz, int) and dz == 0 else rem(z + (Z + dz), Z)
        return (to_z * (2 * X) + to_x * 2 + rem(to_y, 2), div(to_y, 2) * 2 + core)

    mate = at(dy=1 - 2 * q)
    twin = at(core=1 - c)

    def copy_to(src, dst, sems, device):
        return pltpu.make_async_remote_copy(
            src_ref=src, dst_ref=dst, send_sem=sems.at[0], recv_sem=sems.at[1],
            device_id=device, device_id_type=MESH,
        )

    def send(*args):
        copy = copy_to(*args)
        copy.start()
        sent.append(copy)
        return copy

    def each(n, body, start=0):
        def step(i, carry):
            body(i)
            return carry

        lax.fori_loop(start, n, step, 0)

    mine = pl.ds(pl.multiple_of(q * HALF, 128), HALF)
    theirs = pl.ds(pl.multiple_of(p * HALF, 128), HALF)

    def a_at(x, q, start=0, size=ROWS):
        return a_all.at[q, pl.ds(pl.multiple_of(x * ROWS + start, 16), size)]

    def b_at(z, q, start=0, size=COLS):
        return b_all.at[pl.ds(pl.multiple_of((z * 2 + q) * COLS + start, 16), size)]

    loads = [
        pltpu.make_async_copy(w_hbm.at[:, mine], b_at(z, q), load_sem.at[0]),
        pltpu.make_async_copy(gate_hbm.at[:, theirs], gate.at[1], load_sem.at[1]),
        pltpu.make_async_copy(up_hbm.at[:, theirs], up.at[1], load_sem.at[2]),
        pltpu.make_async_copy(gate_hbm.at[:, mine], gate.at[0], load_sem.at[3]),
        pltpu.make_async_copy(up_hbm.at[:, mine], up.at[0], load_sem.at[4]),
    ]
    for load in loads:
        load.start()

    barrier = pltpu.get_barrier_semaphore()

    def greet(device):
        pl.semaphore_signal(barrier, inc=1, device_id=device, device_id_type=MESH)

    up_z, down_z = at(dz=1), at(dz=-1)
    greet(up_z)
    greet(down_z)
    greet(at(dy=1))
    greet(at(dy=-1))
    greet(at(1))
    greet(at(3))
    greet(twin)
    def act(i, dst):
        def rows(r):
            at_rows = pl.ds(pl.multiple_of(r * 16, 16), 16)
            g = gate[i, at_rows].astype(jnp.float32)
            h = g / (1.0 + jnp.exp(-g)) * up[i, at_rows].astype(jnp.float32)
            dst[at_rows] = h.astype(jnp.bfloat16)

        each(ROWS // 16, rows)

    pl.semaphore_wait(barrier, 7)
    for dy in (1, -1):
        pl.semaphore_signal(relay, inc=1, device_id=at(dy=dy), device_id_type=MESH)

    cut = COLS // 2
    w_swap = [
        send(w_hbm.at[pl.ds(i * cut, cut), theirs], b_at(z, q, i * cut, cut), wx_sem.at[i], mate)
        for i in range(2)
    ]

    def z_hop(step, piece):
        who = p if piece > 1 else q
        far, size = (2, cut // 2) if step == 3 else (step, cut)
        start = piece % 2 * cut
        ahead = b_at(rem(z + (Z - far), Z), who, start, size)
        behind = b_at(rem(z + far, Z), who, start + cut - size, size)
        return [
            send(ahead, ahead, z_sem.at[0, step, piece], at(dz=2) if step == 3 else up_z),
            send(behind, behind, z_sem.at[1, step, piece], at(dz=-2) if step == 3 else down_z),
        ]

    right, left = at(1), at(3)

    def x_hop(piece):
        src = a_at(x, p if piece > 1 else q, piece % 2 * 64, 64)
        return [send(src, src, x_sem.at[i, piece], d) for i, d in enumerate((right, left))]

    def x_on(piece):
        i = piece % 2
        src = a_at(rem(x + (3 if i == 0 else 1), X), p if piece > 1 else q, i * 64, 64)
        return [send(src, src, x_sem.at[2, piece], right if i == 0 else left)]

    def landed(copies):
        for copy in copies:
            copy.wait_recv()

    zs, xs, xo = {}, {}, {}
    loads[0].wait()
    for i in (0, 1):
        zs[0, i] = z_hop(0, i)
    loads[1].wait()
    loads[2].wait()
    act(1, h_send)
    a_swap = [
        send(h_send.at[pl.ds(i * 64, 64)], a_at(x, q, i * 64, 64), ax_sem.at[i], mate) for i in range(2)
    ]
    loads[3].wait()
    loads[4].wait()
    act(0, a_at(x, q))
    for i in (0, 1):
        xs[i] = x_hop(i)
    for i in (2, 3):
        w_swap[i - 2].wait_recv()
        zs[0, i] = z_hop(0, i)
    for i in (0, 1):
        landed(zs[0, i])
        zs[1, i] = z_hop(1, i)
    pl.semaphore_wait(relay, 2)
    for i in (2, 3):
        a_swap[i - 2].wait_recv()
        xs[i] = x_hop(i)
    for i in (2, 3):
        landed(zs[0, i])
        zs[1, i] = z_hop(1, i)
    for i in (0, 1):
        landed(xs[i])
        xo[i] = x_on(i)
    for i in (0, 1):
        landed(zs[1, i])
        zs[2, i] = z_hop(2, i)
        zs[3, i] = z_hop(3, i)
    for i in (2, 3):
        landed(xs[i])
        xo[i] = x_on(i)
    for i in (2, 3):
        landed(zs[1, i])
        zs[2, i] = z_hop(2, i)
        zs[3, i] = z_hop(3, i)
    near_z = [copy for i in range(4) for copy in zs[2, i]]
    far_z = [copy for i in range(4) for copy in zs[3, i]]
    for i in range(4):
        landed(xo[i])

    def core_copy(to):
        return copy_to(part.at[1 - c, to], other.at[to], c_sem.at[to], twin)

    def product(i):
        pl.when(i == 5)(lambda: landed(near_z))
        pl.when(i == 7)(lambda: landed(far_z))
        odd = rem(i, 2)
        zz = rem(z + odd * div(i + 1, 2) + (1 - odd) * (Z - div(i, 2)), Z)
        owner, to = rem(zz, 2), div(zz, 2) * 2
        b = b_all[pl.ds(pl.multiple_of(zz * 128, 128), 128)]

        def block(j):
            part[owner, to + j] = lax.dot_general(
                a_all[j], b, (((1,), (1,)), ((), ())), preferred_element_type=jnp.float32
            )

        each(2, block)

        @pl.when(owner != c)
        def _():
            core_copy(to).start()
            core_copy(to + 1).start()

    half = 2 * ROWS

    def settle(offset):
        to = rem(y + Y + offset, Y)
        core_copy(to).wait_recv()
        return to

    def pack(to, dst, start=0, stop=X, extra=()):
        def chunk(k):
            rows = pl.ds(pl.multiple_of(k * ROWS, ROWS), ROWS)
            v = part[c, to, rows] + other[to, rows]
            for e in extra:
                v = v + e[rows].astype(jnp.float32)
            dst[rows] = v.astype(jnp.bfloat16)

        each(stop, chunk, start)

    def far(i):
        rows = pl.ds(i * half, half)
        return copy_to(s_buf.at[0, rows], r_buf.at[0, rows], y_sem.at[i], at(dy=-2 if i else 2))

    def near(i):
        return copy_to(s_buf.at[1 + i], r_buf.at[1 + i], y_sem.at[2 + i], at(dy=-1 if i else 1))

    def when_due(offset, batch, body):
        to = rem(y + Y + offset, Y)
        dz = rem(div(to, 2) * 2 + c + (Z + 2) - z, Z)
        late = (dz > 4).astype(jnp.int32)

        @pl.when(late == batch)
        def _():
            body(to)

    def last(offset, k):
        rows = pl.ds(pl.multiple_of(rem(x + k, X) * ROWS, ROWS), ROWS)
        return copy_to(f_buf.at[offset + 2, rows], fin.at[offset + 2, x], f_sem.at[offset + 2, k], at(k, offset))

    def final(offset):
        if offset:
            last(offset, 2).start()
        for k in (1, 3) if offset else (2, 1, 3):
            last(offset, k).start()
        if offset:
            last(offset, 0).start()

    def send_far(to):
        settle(4)
        pack(to, s_buf.at[0])
        far(0).start()
        far(1).start()

    def send_near(i, offset):
        def body(to):
            settle(offset)
            pack(to, s_buf.at[1 + i])
            near(i).start()

        return body

    def send_own(offset):
        def body(to):
            settle(offset)
            pack(to, f_buf.at[offset + 2])
            final(offset)

        return body

    def send_sum(i, offset):
        def body(to):
            settle(offset)
            far(i).wait_recv()
            near(i).wait_recv()
            pack(to, f_buf.at[offset + 2], 2 * i, 2 * i + 2, (r_buf.at[0], r_buf.at[1 + i]))
            pack(to, f_buf.at[offset + 2], 2 - 2 * i, 4 - 2 * i, (r_buf.at[1 + i],))
            final(offset)

        return body

    def batch(b):
        each(5 + 3 * b, product, 5 * b)
        when_due(4, b, send_far)
        when_due(3, b, send_near(0, 3))
        when_due(-3, b, send_near(1, -3))
        for offset in (1, -1, 0):
            when_due(offset, b, send_own(offset))

    each(2, batch)

    def sums(b):
        when_due(2, b, send_sum(0, 2))
        when_due(-2, b, send_sum(1, -2))

    each(2, sums)
    fin[2, x] = f_buf[2, pl.ds(pl.multiple_of(x * ROWS, ROWS), ROWS)]
    for copy in sent + [far(0), far(1), near(0), near(1)]:
        copy.wait_send()
    each(Y, lambda i: core_copy(i).wait_send())
    for offset in (0, 1, -1, 2, -2):
        each(X, lambda k: last(offset, k).wait_send(), 0 if offset else 1)
    for offset in (0, 1, -1, 2, -2):
        each(X, lambda k: last(offset, k).wait_recv(), 0 if offset else 1)

    def add_up(i):
        total = fin[0, i].astype(jnp.float32)
        for j in range(1, 5):
            total = total + fin[j, i].astype(jnp.float32)
        out_ref[:, pl.ds(pl.multiple_of(i * 128, 128), 128)] = total.astype(jnp.bfloat16)

    each(X, add_up)


def shards(gate_pre, up_pre, down_weight):
    dma = pltpu.SemaphoreType.DMA
    bf16, f32 = jnp.bfloat16, jnp.float32
    return pl.pallas_call(
        kernel,
        out_shape=jax.ShapeDtypeStruct((ROWS, 512), bf16),
        in_specs=[pl.BlockSpec(memory_space=pl.ANY)] * 3,
        out_specs=pl.BlockSpec(memory_space=pltpu.VMEM),
        scratch_shapes=[
            pltpu.VMEM((2, ROWS, HALF), bf16),
            pltpu.VMEM((2, ROWS, HALF), bf16),
            pltpu.VMEM((ROWS, HALF), bf16),
            pltpu.VMEM((2, X * ROWS, HALF), bf16),
            pltpu.VMEM((Z * 2 * COLS, HALF), bf16),
            pltpu.VMEM((2, Y, X * ROWS, 128), f32),
            pltpu.VMEM((Y, X * ROWS, 128), f32),
            pltpu.VMEM((3, X * ROWS, 128), bf16),
            pltpu.VMEM((3, X * ROWS, 128), bf16),
            pltpu.VMEM((5, X * ROWS, 128), bf16),
            pltpu.VMEM((5, X, ROWS, 128), bf16),
            dma((5,)),
            dma((2, 2)),
            dma((2, 2)),
            dma((3, 4, 2)),
            dma((2, 4, 4, 2)),
            dma((Y, 2)),
            dma((4, 2)),
            dma((5, X, 2)),
            pltpu.SemaphoreType.REGULAR,
        ],
        compiler_params=pltpu.CompilerParams(
            collective_id=0, has_side_effects=True, vmem_limit_bytes=55000 * 1024
        ),
        name="down_projection",
    )(gate_pre, up_pre, down_weight.T)


def solution(mesh):
    return jax.shard_map(
        shards,
        mesh=mesh,
        in_specs=(P("fsdp", "tp"), P("fsdp", "tp"), P("tp", "fsdp")),
        out_specs=P("fsdp", "tp"),
        check_vma=False,
    )
```

```python
import jax
import jax.numpy as jnp
from jax import lax
from jax.experimental import pallas as pl
from jax.experimental.pallas import tpu as pltpu
from jax.sharding import PartitionSpec as P

MESH = pl.DeviceIdType.MESH
X, Y, Z = 4, 8, 8
ROWS, COLS, HALF = 128, 64, 896


def kernel(
    gate_hbm, up_hbm, w_hbm, out_ref,
    gate, up, h_send, a_all, b_all, part, other, s_buf, r_buf, f_buf, fin,
    load_sem, wx_sem, ax_sem, x_sem, z_sem, c_sem, y_sem, f_sem, relay,
):
    rem, div = lax.rem, lax.div
    f, t = lax.axis_index("fsdp"), lax.axis_index("tp")
    x, q, z = rem(div(f, 2), X), rem(f, 2), div(f, 2 * X)
    y, c = div(t, 2) * 2 + q, rem(t, 2)
    p = 1 - q
    sent = []

    def at(dx=0, dy=0, dz=0, core=c):
        to_x = x if isinstance(dx, int) and dx == 0 else rem(x + (X + dx), X)
        to_y = y if isinstance(dy, int) and dy == 0 else rem(y + (Y + dy), Y)
        to_z = z if isinstance(dz, int) and dz == 0 else rem(z + (Z + dz), Z)
        return (to_z * (2 * X) + to_x * 2 + rem(to_y, 2), div(to_y, 2) * 2 + core)

    mate = at(dy=1 - 2 * q)
    twin = at(core=1 - c)

    def copy_to(src, dst, sems, device):
        return pltpu.make_async_remote_copy(
            src_ref=src, dst_ref=dst, send_sem=sems.at[0], recv_sem=sems.at[1],
            device_id=device, device_id_type=MESH,
        )

    def send(*args):
        copy = copy_to(*args)
        copy.start()
        sent.append(copy)
        return copy

    def each(n, body, start=0):
        def step(i, carry):
            body(i)
            return carry

        lax.fori_loop(start, n, step, 0)

    mine = pl.ds(pl.multiple_of(q * HALF, 128), HALF)
    theirs = pl.ds(pl.multiple_of(p * HALF, 128), HALF)

    def a_at(x, q, start=0, size=ROWS):
        return a_all.at[q, pl.ds(pl.multiple_of(x * ROWS + start, 16), size)]

    def b_at(z, q, start=0, size=COLS):
        return b_all.at[pl.ds(pl.multiple_of((z * 2 + q) * COLS + start, 16), size)]

    loads = [
        pltpu.make_async_copy(w_hbm.at[:, mine], b_at(z, q), load_sem.at[0]),
        pltpu.make_async_copy(gate_hbm.at[:, theirs], gate.at[1], load_sem.at[1]),
        pltpu.make_async_copy(up_hbm.at[:, theirs], up.at[1], load_sem.at[2]),
        pltpu.make_async_copy(gate_hbm.at[:, mine], gate.at[0], load_sem.at[3]),
        pltpu.make_async_copy(up_hbm.at[:, mine], up.at[0], load_sem.at[4]),
    ]
    for load in loads:
        load.start()

    barrier = pltpu.get_barrier_semaphore()

    def greet(device):
        pl.semaphore_signal(barrier, inc=1, device_id=device, device_id_type=MESH)

    up_z, down_z = at(dz=1), at(dz=-1)
    greet(up_z)
    greet(down_z)
    greet(at(dy=1))
    greet(at(dy=-1))
    greet(at(1))
    greet(at(3))
    greet(twin)
    def act(i, dst):
        def rows(r):
            at_rows = pl.ds(pl.multiple_of(r * 16, 16), 16)
            g = gate[i, at_rows].astype(jnp.float32)
            h = g / (1.0 + jnp.exp(-g)) * up[i, at_rows].astype(jnp.float32)
            dst[at_rows] = h.astype(jnp.bfloat16)

        each(ROWS // 16, rows)

    pl.semaphore_wait(barrier, 7)
    for dy in (1, -1):
        pl.semaphore_signal(relay, inc=1, device_id=at(dy=dy), device_id_type=MESH)

    cut = COLS // 2
    w_swap = [
        send(w_hbm.at[pl.ds(i * cut, cut), theirs], b_at(z, q, i * cut, cut), wx_sem.at[i], mate)
        for i in range(2)
    ]

    def z_hop(step, piece):
        who = p if piece > 1 else q
        far, size = (2, cut // 2) if step == 3 else (step, cut)
        start = piece % 2 * cut
        ahead = b_at(rem(z + (Z - far), Z), who, start, size)
        behind = b_at(rem(z + far, Z), who, start + cut - size, size)
        return [
            send(ahead, ahead, z_sem.at[0, step, piece], at(dz=2) if step == 3 else up_z),
            send(behind, behind, z_sem.at[1, step, piece], at(dz=-2) if step == 3 else down_z),
        ]

    right, left = at(1), at(3)

    def x_piece(piece):
        return (piece * 64, 64, piece) if piece < 2 else ((piece - 2) * 32, 32, (piece - 2) // 2)

    def x_hop(piece):
        start, size, _ = x_piece(piece)
        src = a_at(x, p if piece > 1 else q, start, size)
        return [send(src, src, x_sem.at[i, piece], d) for i, d in enumerate((right, left))]

    def x_on(piece):
        start, size, way = x_piece(piece)
        src = a_at(rem(x + (1 if way else 3), X), p if piece > 1 else q, start, size)
        return [send(src, src, x_sem.at[2, piece], left if way else right)]

    def landed(copies):
        for copy in copies:
            copy.wait_recv()

    zs, xs, xo = {}, {}, {}
    loads[0].wait()
    for i in (0, 1):
        zs[0, i] = z_hop(0, i)
    loads[1].wait()
    loads[2].wait()
    act(1, h_send)
    a_swap = [
        send(h_send.at[pl.ds(i * 32, 32)], a_at(x, q, i * 32, 32), ax_sem.at[i], mate) for i in range(4)
    ]
    loads[3].wait()
    loads[4].wait()
    act(0, a_at(x, q))
    for i in (0, 1):
        xs[i] = x_hop(i)
    for i in (2, 3):
        w_swap[i - 2].wait_recv()
        zs[0, i] = z_hop(0, i)
    for i in (0, 1):
        landed(zs[0, i])
        zs[1, i] = z_hop(1, i)
    pl.semaphore_wait(relay, 2)
    for i in range(2, 6):
        a_swap[i - 2].wait_recv()
        xs[i] = x_hop(i)
    for i in (2, 3):
        landed(zs[0, i])
        zs[1, i] = z_hop(1, i)
    for i in (0, 1):
        landed(xs[i])
        xo[i] = x_on(i)
    for i in (0, 1):
        landed(zs[1, i])
        zs[2, i] = z_hop(2, i)
        zs[3, i] = z_hop(3, i)
    for i in range(2, 6):
        landed(xs[i])
        xo[i] = x_on(i)
    for i in (2, 3):
        landed(zs[1, i])
        zs[2, i] = z_hop(2, i)
        zs[3, i] = z_hop(3, i)
    near_z = [copy for i in range(4) for copy in zs[2, i]]
    far_z = [copy for i in range(4) for copy in zs[3, i]]
    for i in range(6):
        landed(xo[i])

    def core_copy(to):
        return copy_to(part.at[1 - c, to], other.at[to], c_sem.at[to], twin)

    def product(i):
        pl.when(i == 5)(lambda: landed(near_z))
        pl.when(i == 7)(lambda: landed(far_z))
        odd = rem(i, 2)
        zz = rem(z + odd * div(i + 1, 2) + (1 - odd) * (Z - div(i, 2)), Z)
        owner, to = rem(zz, 2), div(zz, 2) * 2
        b = b_all[pl.ds(pl.multiple_of(zz * 128, 128), 128)]

        def block(j):
            part[owner, to + j] = lax.dot_general(
                a_all[j], b, (((1,), (1,)), ((), ())), preferred_element_type=jnp.float32
            )

        each(2, block)

        @pl.when(owner != c)
        def _():
            core_copy(to).start()
            core_copy(to + 1).start()

    half = 2 * ROWS

    def settle(offset):
        to = rem(y + Y + offset, Y)
        core_copy(to).wait_recv()
        return to

    def pack(to, dst, start=0, stop=X, extra=()):
        def chunk(k):
            rows = pl.ds(pl.multiple_of(k * ROWS, ROWS), ROWS)
            v = part[c, to, rows] + other[to, rows]
            for e in extra:
                v = v + e[rows].astype(jnp.float32)
            dst[rows] = v.astype(jnp.bfloat16)

        each(stop, chunk, start)

    def far(i):
        rows = pl.ds(i * half, half)
        return copy_to(s_buf.at[0, rows], r_buf.at[0, rows], y_sem.at[i], at(dy=-2 if i else 2))

    def near(i):
        return copy_to(s_buf.at[1 + i], r_buf.at[1 + i], y_sem.at[2 + i], at(dy=-1 if i else 1))

    def when_due(offset, batch, body):
        to = rem(y + Y + offset, Y)
        dz = rem(div(to, 2) * 2 + c + (Z + 2) - z, Z)
        late = (dz > 4).astype(jnp.int32)

        @pl.when(late == batch)
        def _():
            body(to)

    def last(offset, k):
        rows = pl.ds(pl.multiple_of(rem(x + k, X) * ROWS, ROWS), ROWS)
        return copy_to(f_buf.at[offset + 2, rows], fin.at[offset + 2, x], f_sem.at[offset + 2, k], at(k, offset))

    def final(offset):
        if offset:
            last(offset, 2).start()
        for k in (1, 3) if offset else (2, 1, 3):
            last(offset, k).start()
        if offset:
            last(offset, 0).start()

    def send_far(to):
        settle(4)
        pack(to, s_buf.at[0])
        far(0).start()
        far(1).start()

    def send_near(i, offset):
        def body(to):
            settle(offset)
            pack(to, s_buf.at[1 + i])
            near(i).start()

        return body

    def send_own(offset):
        def body(to):
            settle(offset)
            pack(to, f_buf.at[offset + 2])
            final(offset)

        return body

    def send_sum(i, offset):
        def body(to):
            settle(offset)
            far(i).wait_recv()
            near(i).wait_recv()
            pack(to, f_buf.at[offset + 2], 2 * i, 2 * i + 2, (r_buf.at[0], r_buf.at[1 + i]))
            pack(to, f_buf.at[offset + 2], 2 - 2 * i, 4 - 2 * i, (r_buf.at[1 + i],))
            final(offset)

        return body

    def batch(b):
        each(5 + 3 * b, product, 5 * b)
        when_due(4, b, send_far)
        when_due(3, b, send_near(0, 3))
        when_due(-3, b, send_near(1, -3))
        for offset in (1, -1, 0):
            when_due(offset, b, send_own(offset))

    each(2, batch)

    def sums(b):
        when_due(2, b, send_sum(0, 2))
        when_due(-2, b, send_sum(1, -2))

    each(2, sums)
    fin[2, x] = f_buf[2, pl.ds(pl.multiple_of(x * ROWS, ROWS), ROWS)]
    for copy in sent + [far(0), far(1), near(0), near(1)]:
        copy.wait_send()
    each(Y, lambda i: core_copy(i).wait_send())
    for offset in (0, 1, -1, 2, -2):
        each(X, lambda k: last(offset, k).wait_send(), 0 if offset else 1)
    for offset in (0, 1, -1, 2, -2):
        each(X, lambda k: last(offset, k).wait_recv(), 0 if offset else 1)

    def add_up(i):
        total = fin[0, i].astype(jnp.float32)
        for j in range(1, 5):
            total = total + fin[j, i].astype(jnp.float32)
        out_ref[:, pl.ds(pl.multiple_of(i * 128, 128), 128)] = total.astype(jnp.bfloat16)

    each(X, add_up)


def shards(gate_pre, up_pre, down_weight):
    dma = pltpu.SemaphoreType.DMA
    bf16, f32 = jnp.bfloat16, jnp.float32
    return pl.pallas_call(
        kernel,
        out_shape=jax.ShapeDtypeStruct((ROWS, 512), bf16),
        in_specs=[pl.BlockSpec(memory_space=pl.ANY)] * 3,
        out_specs=pl.BlockSpec(memory_space=pltpu.VMEM),
        scratch_shapes=[
            pltpu.VMEM((2, ROWS, HALF), bf16),
            pltpu.VMEM((2, ROWS, HALF), bf16),
            pltpu.VMEM((ROWS, HALF), bf16),
            pltpu.VMEM((2, X * ROWS, HALF), bf16),
            pltpu.VMEM((Z * 2 * COLS, HALF), bf16),
            pltpu.VMEM((2, Y, X * ROWS, 128), f32),
            pltpu.VMEM((Y, X * ROWS, 128), f32),
            pltpu.VMEM((3, X * ROWS, 128), bf16),
            pltpu.VMEM((3, X * ROWS, 128), bf16),
            pltpu.VMEM((5, X * ROWS, 128), bf16),
            pltpu.VMEM((5, X, ROWS, 128), bf16),
            dma((5,)),
            dma((2, 2)),
            dma((4, 2)),
            dma((3, 6, 2)),
            dma((2, 4, 4, 2)),
            dma((Y, 2)),
            dma((4, 2)),
            dma((5, X, 2)),
            pltpu.SemaphoreType.REGULAR,
        ],
        compiler_params=pltpu.CompilerParams(
            collective_id=0, has_side_effects=True, vmem_limit_bytes=55000 * 1024
        ),
        name="down_projection",
    )(gate_pre, up_pre, down_weight.T)


def solution(mesh):
    return jax.shard_map(
        shards,
        mesh=mesh,
        in_specs=(P("fsdp", "tp"), P("fsdp", "tp"), P("tp", "fsdp")),
        out_specs=P("fsdp", "tp"),
        check_vma=False,
    )
```
